32 devices in a mesh: dp: 8 (over z, x), outer: 4 (over y, core).
Axes of the slice: x: 2, y: 2, z: 4, core: 2. Of those that a mesh axis runs over, the one named last changes fastest.
Arguments:
- partials: bfloat16 [4, 8, 2, 16, 8192], P('outer', 'dp'), may hold values from -3500 to 3500, as said below
- master: float32 [2, 16, 8192], P(None, 'dp'), may hold values from -6 to 6
- m_codes: bfloat16 [2, 16, 8192], P(None, 'dp'), may hold values from -1 to 1
- v_codes: bfloat16 [2, 16, 8192], P(None, 'dp'), may hold values from 0.049804688 to 1
- m_scales: float32 [2, 16, 4], P(None, 'dp'), may hold values from 0.0001 to 0.001
- v_scales: float32 [2, 16, 4], P(None, 'dp'), may hold values from 1e-08 to 1e-07
Outputs:
- new_master: float32 [2, 16, 8192], P(None, 'dp')
- new_m_codes: bfloat16 [2, 16, 8192], P(None, 'dp')
- new_v_codes: bfloat16 [2, 16, 8192], P(None, 'dp')
- new_m_scales: float32 [2, 16, 4], P(None, 'dp')
- new_v_scales: float32 [2, 16, 4], P(None, 'dp')
- weights: bfloat16 [2, 16, 8192], replicated
The draws below stay inside these ranges and needn't reach their ends.
Inputs may be any that keep to these rules, and one draw needn't show every extreme that they name: Gradient partials of real values; entries vary from row to row and column to column.
All inputs are finite; a program needn't handle non-finite values. Where the reference program divides by a largest or mean magnitude, that divisor is 1e-20 or more.
Results may differ from the reference program's by a relative error of at most 0.0004.
Values may be sent and summed in bfloat16 or wider, within the bound.
No kernel may reach another device: no remote copies, remote signals or barrier semaphores. Data moves between devices by JAX's collectives and lax.ppermute only.
A program may use at most 64 MiB of HBM per device.

```python
import math
import jax
import jax.numpy as jnp
from jax import lax

D = 8192
BLOCK = 2048
STEP = 10
V = 16
REPLICAS = 8
GROUPS = 4


def draw_partials(key, part):
    keys = jax.random.split(jax.random.fold_in(key, 17), 3)
    shape_full = (GROUPS, REPLICAS, 2, V, D)
    ramp = 1.0 + 2.0 * jnp.arange(V, dtype=jnp.float32) / max(V - 1, 1)
    row_scale = jnp.exp(jax.random.uniform(keys[1], (2, V, 1), jnp.float32) * math.log(10.0)) * ramp[None, :, None]
    col_scale = jnp.exp(jax.random.uniform(keys[2], (2, 1, D), jnp.float32) * math.log(10.0))
    base = jnp.clip(jax.random.normal(keys[0], shape_full, jnp.float32), -6.0, 6.0)
    return (base * row_scale[None, None] * col_scale[None, None]).astype(jnp.bfloat16)


def shard_levels(rng, dims, shards, low, top_value):
    factor_of, own = 1.0, jax.random.fold_in(rng, 6)
    for position, shards_of in shards:
        heights = jnp.exp(jax.random.uniform(jax.random.fold_in(own, position), (shards_of,), jnp.float32, low / len(shards), top_value / len(shards)))
        factor_of = factor_of * jnp.repeat(heights, dims[position] // shards_of).reshape([-1 if axis == position else 1 for axis in range(len(dims))])
    return factor_of


def centred(own_key, dims, scale, limit, cuts=(), kind=jnp.bfloat16):
    loudness = shard_levels(own_key, dims, cuts, -0.22, 0.18) if cuts else 1.0
    result = jax.random.normal(own_key, dims, jnp.float32) * scale * loudness
    return jnp.minimum(jnp.maximum(result, -limit), limit).astype(kind)


def setup_inputs(seed: int = 0) -> dict:
    streams_of = jax.random.split(jax.random.key(seed), 7)
    return {
        "partials": draw_partials(jax.random.fold_in(streams_of[6], 71), 0),
        "master": centred(streams_of[1], (2, V, D), 1.0, 6.0, ((1, 8),), jnp.float32),
        "m_codes": jnp.clip(jax.random.uniform(streams_of[2], (2, V, D), jnp.float32, -1.0, 1.0) * shard_levels(streams_of[2], (2, V, D), ((1, 8),), -0.4, 0.0), -1.0, 1.0).astype(jnp.bfloat16),
        "v_codes": jnp.clip(0.049804688 + 0.9501953 * jax.random.uniform(streams_of[3], (2, V, D), jnp.float32) ** shard_levels(streams_of[3], (2, V, D), ((1, 8),), -0.2, 0.2), 0.049804688, 1.0).astype(jnp.bfloat16),
        "m_scales": jnp.clip(jnp.exp(math.log(0.001) - 2.3025852 * jax.random.uniform(streams_of[4], (2, V, D // BLOCK), jnp.float32) ** shard_levels(streams_of[4], (2, V, D // BLOCK), ((1, 8),), -0.2, 0.2)), 0.0001, 0.001),
        "v_scales": jnp.clip(jnp.exp(math.log(1.0000000116860974e-07) - 2.3025851 * jax.random.uniform(streams_of[5], (2, V, D // BLOCK), jnp.float32) ** shard_levels(streams_of[5], (2, V, D // BLOCK), ((1, 8),), -0.2, 0.2)), 9.99999993922529e-09, 1.0000000116860974e-07),
    }


def adam_blocks(gradient, master, m_codes, v_codes, m_scales, v_scales, clip_factor):
    count = gradient.shape[0]
    rows = gradient.shape[1]
    blocks = gradient.shape[2] // BLOCK
    shape_four = (count, rows, blocks, BLOCK)
    moment = m_codes.astype(jnp.float32).reshape(shape_four) * m_scales[..., None]
    second = v_codes.astype(jnp.float32).reshape(shape_four) * v_scales[..., None]
    scaled = clip_factor * gradient.reshape(shape_four)
    moment = 0.9 * moment + 0.1 * scaled
    second = 0.95 * second + 0.05 * scaled * scaled
    update = moment / (1.0 - 0.9 ** STEP) / (jnp.sqrt(second / (1.0 - 0.95 ** STEP)) + 1e-08)
    fresh = master - 0.01 * update.reshape(master.shape)
    m_top = lax.optimization_barrier(jnp.max(jnp.abs(moment), axis=3)) + 1e-20
    v_top = lax.optimization_barrier(jnp.max(jnp.abs(second), axis=3)) + 1e-20
    m_next = (moment / m_top[..., None]).astype(jnp.bfloat16).reshape(master.shape)
    v_next = (second / v_top[..., None]).astype(jnp.bfloat16).reshape(master.shape)
    return (fresh, m_next, v_next, m_top, v_top, fresh.astype(jnp.bfloat16))

def reference(partials, master, m_codes, v_codes, m_scales, v_scales):

    def add_group(total, group):
        return (total + lax.optimization_barrier(jnp.sum(group.astype(jnp.float32), axis=0)), None)
    start_sum = jnp.zeros(partials.shape[2:], jnp.float32)
    gradient, _ = lax.scan(add_group, start_sum, partials)
    norm_value = jnp.sqrt(jnp.sum(gradient * gradient))
    clip_factor = 1.0 / jnp.maximum(norm_value, 1.0)
    return adam_blocks(gradient, master, m_codes, v_codes, m_scales, v_scales, clip_factor)
```

```python
import jax
import jax.numpy as jnp
from jax import lax
from jax.sharding import PartitionSpec as P

BLOCK = 2048
STEP = 10


def adam_blocks(gradient, master, m_codes, v_codes, m_scales, v_scales, clip_factor):
    count, rows, width = gradient.shape
    shape_four = (count, rows, width // BLOCK, BLOCK)
    moment = m_codes.astype(jnp.float32).reshape(shape_four) * m_scales[..., None]
    second = v_codes.astype(jnp.float32).reshape(shape_four) * v_scales[..., None]
    scaled = clip_factor * gradient.reshape(shape_four)
    moment = 0.9 * moment + 0.1 * scaled
    second = 0.95 * second + 0.05 * scaled * scaled
    update = moment / (1.0 - 0.9**STEP) / (jnp.sqrt(second / (1.0 - 0.95**STEP)) + 1e-08)
    fresh = master - 0.01 * update.reshape(master.shape)
    m_top = jnp.max(jnp.abs(moment), axis=3) + 1e-20
    v_top = jnp.max(jnp.abs(second), axis=3) + 1e-20
    m_next = (moment / m_top[..., None]).astype(jnp.bfloat16).reshape(master.shape)
    v_next = (second / v_top[..., None]).astype(jnp.bfloat16).reshape(master.shape)
    return (fresh, m_next, v_next, m_top, v_top, fresh.astype(jnp.bfloat16))


def flip(value, axis, size, bit):
    return lax.ppermute(value, axis, [(i, i ^ bit) for i in range(size)])


def make_body(dp_n, outer_n):
    both = ("dp", "outer")

    def body(partials, master, m_codes, v_codes, m_scales, v_scales):
        own = partials[0, 0]
        count, rows_all, width = own.shape
        rows = rows_all // dp_n
        part = width // outer_n
        outer_at = lax.axis_index("outer")
        pieces = own.reshape(count, dp_n, rows, outer_n, part)
        pieces = pieces.transpose(1, 3, 0, 2, 4).reshape(dp_n * outer_n, count * rows, part)
        got = lax.all_to_all(pieces, both, 0, 0, tiled=True)
        piece = jnp.sum(got.astype(jnp.float32), axis=0)
        square = jnp.sum(piece * piece)
        held = piece[None]
        bit = 1
        while bit < outer_n:
            other = flip(held, "outer", outer_n, bit)
            held = jnp.concatenate([held, other], axis=0)
            bit *= 2
        squares = lax.all_to_all(
            jnp.broadcast_to(square, (dp_n * outer_n, 8, 128)), both, 0, 0, tiled=True
        )
        total = jnp.sum(squares[:, 0, 0])
        clip_factor = 1.0 / jnp.maximum(jnp.sqrt(total), 1.0)
        order = [lax.dynamic_index_in_dim(held, j ^ outer_at, 0, keepdims=False) for j in range(outer_n)]
        gradient = jnp.stack(order, axis=1).reshape(count, rows, width)
        results = adam_blocks(gradient, master, m_codes, v_codes, m_scales, v_scales, clip_factor)
        fresh, m_next, v_next, m_top, v_top, rounded = results
        side = outer_at % 2
        mine = lax.dynamic_index_in_dim(rounded, side, 0, keepdims=False)
        mine = lax.all_to_all(
            jnp.broadcast_to(mine, (dp_n, rows, width)), "dp", 0, 0, tiled=True
        ).reshape(rows_all, width)
        other = flip(mine, "outer", outer_n, 1)
        weights = jnp.where(side == 0, jnp.stack([mine, other]), jnp.stack([other, mine]))
        return (fresh, m_next, v_next, m_top, v_top, weights)

    return body


def solution(mesh):
    rows = P(None, "dp", None)
    return jax.shard_map(
        make_body(mesh.shape["dp"], mesh.shape["outer"]),
        mesh=mesh,
        in_specs=(P("outer", "dp", None, None, None), rows, rows, rows, rows, rows),
        out_specs=(rows, rows, rows, rows, rows, P()),
        check_vma=False,
    )
```

```python
import jax
import jax.numpy as jnp
from jax import lax
from jax.experimental import pallas as pl
from jax.experimental.pallas import tpu as pltpu
from jax.sharding import PartitionSpec as P

BLOCK = 2048
STEP = 10
LANES = 128
SUBLANES = 8
NEAR_BYTES = 768 * 1024
BOTH = ("dp", "outer")
FIRST_FIX = 1.0 / (1.0 - 0.9**STEP)
SECOND_FIX = 1.0 / (1.0 - 0.95**STEP)


def sum_kernel(got_ref, piece_ref, square_ref):
    terms = got_ref.shape[0]
    group = 8

    def some(i):
        return jnp.sum(got_ref[pl.ds(i * group, group)].astype(jnp.float32), axis=0)

    total = some(0)
    if terms <= 4 * group:
        for i in range(1, terms // group):
            total = total + some(i)
    else:
        total = lax.fori_loop(1, terms // group, lambda i, held: held + some(i), total)
    piece_ref[...] = total
    lanes = jnp.sum(total * total, axis=0, keepdims=True)
    square_ref[...] = jnp.broadcast_to(lanes[None], square_ref.shape)


def prep_kernel(m_ref, v_ref, ms_ref, vs_ref, m_out_ref, v_out_ref):
    count, rows, blocks = ms_ref.shape
    span = BLOCK // LANES * rows
    for at in range(count):
        for block in range(blocks):
            here = pl.ds(block * span, span)
            for code_ref, scale_ref, decay, out_ref in (
                (m_ref, ms_ref, 0.9, m_out_ref),
                (v_ref, vs_ref, 0.95, v_out_ref),
            ):
                scale = scale_ref[at, :, block : block + 1]
                scale = jnp.concatenate([scale] * (span // rows), axis=0)
                out_ref[at, here, :] = decay * (code_ref[at, here, :].astype(jnp.float32) * scale)


def clip_of(square_ref):
    total = jnp.sum(jnp.sum(square_ref[...], axis=0), axis=1, keepdims=True)
    return 1.0 / jnp.maximum(jnp.sqrt(total), 1.0)


def moments(clip, piece_ref, m_ref, v_ref, at, start, here, span):
    g = clip * piece_ref[pl.ds(start, span), :]
    return m_ref[at, here, :] + 0.1 * g, v_ref[at, here, :] + 0.05 * g * g


def fresh_of(master_ref, at, here, m, v):
    update = (m * FIRST_FIX) / (jnp.sqrt(v * SECOND_FIX) + 1e-08)
    return master_ref[at, here, :] - 0.01 * update


def weight_kernel(square_ref, master_ref, m_ref, v_ref, *refs):
    *piece_refs, out_ref = refs
    outer_at = lax.axis_index("outer")
    side = outer_at % 2
    held = piece_refs[0].shape[0] // master_ref.shape[0]
    clip = clip_of(square_ref)
    for offset, piece_ref in enumerate(piece_refs):
        here = pl.ds(pl.multiple_of((outer_at ^ offset) * held, SUBLANES), held)
        start = pl.multiple_of(side * held, SUBLANES)
        m, v = moments(clip, piece_ref, m_ref, v_ref, side, start, here, held)
        fresh = fresh_of(master_ref, side, here, m, v).astype(jnp.bfloat16)
        out_ref[:, here, :] = jnp.broadcast_to(fresh[None], (out_ref.shape[0],) + fresh.shape)


def state_kernel(rows, square_ref, master_ref, m_ref, v_ref, *refs):
    *piece_refs, fresh_ref, m_next_ref, v_next_ref, m_top_ref, v_top_ref = refs
    outer_at = lax.axis_index("outer")
    count = master_ref.shape[0]
    span = BLOCK // LANES * rows
    held = piece_refs[0].shape[0] // count
    clip = clip_of(square_ref)
    columns = lax.broadcasted_iota(jnp.int32, m_top_ref.shape[1:], 1)

    def top_of(value):
        top = jnp.max(jnp.abs(value).reshape(span // SUBLANES, SUBLANES, LANES), axis=0)
        step = rows
        while step < SUBLANES:
            top = jnp.maximum(top, pltpu.roll(top, step, 0))
            step *= 2
        return jnp.max(top, axis=1, keepdims=True) + 1e-20

    def scaled(value, top):
        tiles = value.reshape(span // SUBLANES, SUBLANES, LANES)
        return (tiles * (1.0 / top)).reshape(span, LANES).astype(jnp.bfloat16)

    for at in range(count):
        m_tops = v_tops = jnp.zeros(m_top_ref.shape[1:], jnp.float32)
        for offset, piece_ref in enumerate(piece_refs):
            for inner in range(held // span):
                block = (outer_at ^ offset) * (held // span) + inner
                here = pl.ds(pl.multiple_of(block * span, SUBLANES), span)
                m, v = moments(clip, piece_ref, m_ref, v_ref, at, at * held + inner * span, here, span)
                fresh_ref[at, here, :] = fresh_of(master_ref, at, here, m, v)
                m_top, v_top = top_of(m), top_of(v)
                m_next_ref[at, here, :] = scaled(m, m_top)
                v_next_ref[at, here, :] = scaled(v, v_top)
                m_tops = jnp.where(columns == block, m_top[:rows], m_tops)
                v_tops = jnp.where(columns == block, v_top[:rows], v_tops)
        m_top_ref[at] = m_tops
        v_top_ref[at] = v_tops


def near(value):
    if value.size * value.dtype.itemsize > NEAR_BYTES:
        return value
    return pltpu.with_memory_space_constraint(value, pltpu.VMEM)


def call(kernel, outs, args, near_in=True, near_out=True):
    def shape_of(shape, dtype):
        plain_shape = jax.ShapeDtypeStruct(shape, dtype)
        small = plain_shape.size * plain_shape.dtype.itemsize <= NEAR_BYTES
        return pltpu.VMEM(shape, dtype) if near_out and small else plain_shape

    spec = pl.BlockSpec(memory_space=pltpu.VMEM)
    return pl.pallas_call(
        kernel,
        out_shape=[shape_of(*out) for out in outs],
        in_specs=[spec] * len(args),
        out_specs=[spec] * len(outs),
    )(*[near(a) if near_in else a for a in args])


def dense(value):
    count, rows, width = value.shape
    tiles = value.reshape(count, rows, width // LANES, LANES).transpose(0, 2, 1, 3)
    return tiles.reshape(count, width // LANES * rows, LANES)


def plain(value, rows):
    count, tall, lanes = value.shape
    tiles = value.reshape(count, tall // rows, rows, lanes).transpose(0, 2, 1, 3)
    return tiles.reshape(count, rows, tall // rows * lanes)


def flip(value, size, bit):
    return lax.ppermute(value, "outer", [(i, i ^ bit) for i in range(size)])


def make_body(dp_n, outer_n):
    f32, bf16 = jnp.float32, jnp.bfloat16

    def body(partials, master, m_codes, v_codes, m_scales, v_scales):
        own = partials[0, 0]
        count, rows_all, width = own.shape
        rows = rows_all // dp_n
        total_n = dp_n * outer_n
        tiles = width // LANES
        part = tiles // outer_n
        tall = (count, tiles * rows, LANES)
        pieces = own.reshape(count, dp_n, rows, outer_n, part, LANES)
        pieces = pieces.transpose(1, 3, 0, 4, 2, 5).reshape(total_n, count * part * rows, LANES)
        got = lax.all_to_all(pieces, BOTH, 0, 0, tiled=True)
        m_part, v_part = call(
            prep_kernel, [(tall, f32), (tall, f32)],
            [dense(m_codes), dense(v_codes), m_scales, v_scales], near_in=False,
        )
        piece, square = call(sum_kernel, [(got.shape[1:], f32), ((total_n, 1, LANES), f32)], [got])
        squares = lax.all_to_all(square, BOTH, 0, 0, tiled=True)
        held = {0: piece}
        bit = outer_n // 2
        while bit:
            for at in list(held):
                held[at ^ bit] = flip(held[at], outer_n, bit)
            bit //= 2
        args = [squares, dense(master), m_part, v_part] + [held[i] for i in range(outer_n)]
        (mine,) = call(weight_kernel, [((dp_n, tiles * rows, LANES), bf16)], args)
        mine = lax.all_to_all(mine, "dp", 0, 0, tiled=True)
        fresh, m_next, v_next, m_top, v_top = call(
            lambda *refs: state_kernel(rows, *refs),
            [(tall, f32), (tall, bf16), (tall, bf16), (m_scales.shape, f32), (v_scales.shape, f32)],
            args, near_out=False,
        )
        mine = mine.reshape(dp_n, tiles, rows, LANES).transpose(0, 2, 1, 3).reshape(rows_all, width)
        other = flip(mine, outer_n, 1)
        side = lax.axis_index("outer") % 2
        weights = jnp.where(side == 0, jnp.stack([mine, other]), jnp.stack([other, mine]))
        return (plain(fresh, rows), plain(m_next, rows), plain(v_next, rows), m_top, v_top, weights)

    return body


def solution(mesh):
    rows = P(None, "dp", None)
    outer_n = mesh.shape["outer"]
    return jax.shard_map(
        make_body(mesh.shape["dp"], outer_n),
        mesh=mesh,
        in_specs=(P("outer", "dp", None, None, None), rows, rows, rows, rows, rows),
        out_specs=(rows, rows, rows, rows, rows, P()),
        check_vma=False,
    )
```

```python
import jax
import jax.numpy as jnp
from jax import lax
from jax.experimental import pallas as pl
from jax.experimental.pallas import tpu as pltpu
from jax.sharding import PartitionSpec as P

BLOCK = 2048
STEP = 10
LANES = 128
SUBLANES = 8
NEAR_BYTES = 768 * 1024
BOTH = ("dp", "outer")
FIRST_FIX = 1.0 / (1.0 - 0.9**STEP)
SECOND_FIX = 1.0 / (1.0 - 0.95**STEP)
SPREAD_EIGHTHS = (2, 7, 6, 1, 0, 5, 3, 4)
SHARE_EIGHTHS = (2, 3, 0, 4, 5, 6, 1, 7)
SHARE_QUARTERS = (3, 1, 0, 2)


def ordered(size, parts):
    if size % len(parts):
        return list(range(size))
    span = size // len(parts)
    return [part * span + i for part in parts for i in range(span)]


def arrange(value, parts):
    if value.shape[0] % len(parts):
        return value
    blocks = jnp.split(value, len(parts), axis=0)
    return jnp.concatenate([blocks[part] for part in parts], axis=0)


def inverse(parts):
    return tuple(parts.index(i) for i in range(len(parts)))


def sum_kernel(count, rows, got_ref, piece_ref, square_ref):
    terms = got_ref.shape[0]
    group = 8

    def some(i):
        return jnp.sum(got_ref[pl.ds(i * group, group)].astype(jnp.float32), axis=0)

    total = some(0)
    if terms <= 4 * group:
        for i in range(1, terms // group):
            total = total + some(i)
    else:
        total = lax.fori_loop(1, terms // group, lambda i, held: held + some(i), total)
    part = total.shape[0] // (count * rows)
    for at in range(count):
        for row in range(rows):
            start = (at * rows + row) * part
            piece_ref[pl.ds(at * rows * part + row, part, stride=rows), :] = total[start : start + part]
    lanes = jnp.sum(total * total, axis=0, keepdims=True)
    square_ref[...] = jnp.broadcast_to(lanes[None], square_ref.shape)


def prep_kernel(m_ref, v_ref, ms_ref, vs_ref, m_out_ref, v_out_ref):
    count, rows, blocks = ms_ref.shape
    span = BLOCK // LANES * rows
    for at in range(count):
        for block in range(blocks):
            here = pl.ds(block * span, span)
            for code_ref, scale_ref, decay, out_ref in (
                (m_ref, ms_ref, 0.9, m_out_ref),
                (v_ref, vs_ref, 0.95, v_out_ref),
            ):
                scale = scale_ref[at, :, block : block + 1]
                scale = jnp.concatenate([scale] * (span // rows), axis=0)
                out_ref[at, here, :] = decay * (code_ref[at, here, :].astype(jnp.float32) * scale)


def clip_of(square_ref):
    total = jnp.sum(jnp.sum(square_ref[...], axis=0), axis=1, keepdims=True)
    return 1.0 / jnp.maximum(jnp.sqrt(total), 1.0)


def moments(clip, piece_ref, m_ref, v_ref, at, start, here, span):
    g = clip * piece_ref[pl.ds(start, span), :]
    return m_ref[at, here, :] + 0.1 * g, v_ref[at, here, :] + 0.05 * g * g


def fresh_of(master_ref, at, here, m, v):
    update = (m * FIRST_FIX) / (jnp.sqrt(v * SECOND_FIX) + 1e-08)
    return master_ref[at, here, :] - 0.01 * update


def weight_kernel(rows, square_ref, master_ref, m_ref, v_ref, *refs):
    *piece_refs, out_ref, hold_ref = refs
    outer_at = lax.axis_index("outer")
    side = outer_at % 2
    held = piece_refs[0].shape[0] // master_ref.shape[0]
    clip = clip_of(square_ref)
    for offset, piece_ref in enumerate(piece_refs):
        here = pl.ds(pl.multiple_of((outer_at ^ offset) * held, SUBLANES), held)
        start = pl.multiple_of(side * held, SUBLANES)
        m, v = moments(clip, piece_ref, m_ref, v_ref, side, start, here, held)
        hold_ref[offset] = fresh_of(master_ref, side, here, m, v)
        part = held // rows
        for row in range(rows):
            fresh = hold_ref[offset, pl.ds(row, part, stride=rows), :].astype(jnp.bfloat16)
            start = row * (out_ref.shape[1] // rows) + (outer_at ^ offset) * part
            there = pl.ds(pl.multiple_of(start, SUBLANES), part)
            out_ref[:, there, :] = jnp.broadcast_to(fresh[None], (out_ref.shape[0],) + fresh.shape)


def half_copy(half_ref, weights_ref, side, sem):
    return pltpu.make_async_copy(half_ref, weights_ref.at[side], sem)


def halves_kernel(mine_ref, other_ref, out_ref, sems):
    side = lax.axis_index("outer") % 2
    copies = [
        half_copy(mine_ref, out_ref, side, sems.at[0]),
        half_copy(other_ref, out_ref, 1 - side, sems.at[1]),
    ]
    for copy in copies:
        copy.start()
    for copy in copies:
        copy.wait()


def state_kernel(rows, square_ref, master_ref, m_ref, v_ref, *refs):
    *piece_refs, fresh_ref, m_next_ref, v_next_ref, m_top_ref, v_top_ref = refs
    outer_at = lax.axis_index("outer")
    count = master_ref.shape[0]
    span = BLOCK // LANES * rows
    held = piece_refs[0].shape[0] // count
    clip = clip_of(square_ref)
    columns = lax.broadcasted_iota(jnp.int32, m_top_ref.shape[1:], 1)

    def top_of(value):
        top = jnp.max(jnp.abs(value).reshape(span // SUBLANES, SUBLANES, LANES), axis=0)
        step = rows
        while step < SUBLANES:
            top = jnp.maximum(top, pltpu.roll(top, step, 0))
            step *= 2
        return jnp.max(top, axis=1, keepdims=True) + 1e-20

    def scaled(value, top):
        tiles = value.reshape(span // SUBLANES, SUBLANES, LANES)
        return (tiles * (1.0 / top)).reshape(span, LANES).astype(jnp.bfloat16)

    for at in range(count):
        m_tops = v_tops = jnp.zeros(m_top_ref.shape[1:], jnp.float32)
        for offset, piece_ref in enumerate(piece_refs):
            for inner in range(held // span):
                block = (outer_at ^ offset) * (held // span) + inner
                here = pl.ds(pl.multiple_of(block * span, SUBLANES), span)
                m, v = moments(clip, piece_ref, m_ref, v_ref, at, at * held + inner * span, here, span)
                fresh_ref[at, here, :] = fresh_of(master_ref, at, here, m, v)
                m_top, v_top = top_of(m), top_of(v)
                m_next_ref[at, here, :] = scaled(m, m_top)
                v_next_ref[at, here, :] = scaled(v, v_top)
                m_tops = jnp.where(columns == block, m_top[:rows], m_tops)
                v_tops = jnp.where(columns == block, v_top[:rows], v_tops)
        m_top_ref[at] = m_tops
        v_top_ref[at] = v_tops


def is_small(value):
    return value.size * value.dtype.itemsize <= NEAR_BYTES


def near(value):
    return pltpu.with_memory_space_constraint(value, pltpu.VMEM) if is_small(value) else value


def call(kernel, outs, args, in_specs=None, out_specs=None, **extra):
    spec = pl.BlockSpec(memory_space=pltpu.VMEM)
    return pl.pallas_call(
        kernel,
        out_shape=outs,
        in_specs=in_specs or [spec] * len(args),
        out_specs=out_specs or [spec] * len(outs),
        **extra,
    )(*args)


def near_shape(shape, dtype):
    far = jax.ShapeDtypeStruct(shape, dtype)
    return pltpu.VMEM(shape, dtype) if is_small(far) else far


def dense(value):
    count, rows, width = value.shape
    tiles = value.reshape(count, rows, width // LANES, LANES).transpose(0, 2, 1, 3)
    return tiles.reshape(count, width // LANES * rows, LANES)


def plain(value, rows):
    count, tall, lanes = value.shape
    tiles = value.reshape(count, tall // rows, rows, lanes).transpose(0, 2, 1, 3)
    return tiles.reshape(count, rows, tall // rows * lanes)


def flip(value, size, bit):
    return lax.ppermute(value, "outer", [(i, i ^ bit) for i in range(size)])


def make_body(dp_n, outer_n):
    f32, bf16 = jnp.float32, jnp.bfloat16

    def body(partials, master, m_codes, v_codes, m_scales, v_scales):
        own = partials[0, 0]
        count, rows_all, width = own.shape
        rows = rows_all // dp_n
        total_n = dp_n * outer_n
        tiles = width // LANES
        part = tiles // outer_n
        tall = (count, tiles * rows, LANES)
        vmem, far = pl.BlockSpec(memory_space=pltpu.VMEM), pl.BlockSpec(memory_space=pl.ANY)
        shape_of = jax.ShapeDtypeStruct
        pieces = own.reshape(count, dp_n, rows, outer_n, part, LANES)
        pieces = arrange(pieces.transpose(1, 3, 0, 2, 4, 5), SHARE_EIGHTHS)
        pieces = arrange(pieces.transpose(1, 0, 2, 3, 4, 5), SHARE_QUARTERS)
        pieces = pieces.reshape(total_n, count * rows * part, LANES)
        share_dp, share_outer = ordered(dp_n, SHARE_EIGHTHS), ordered(outer_n, SHARE_QUARTERS)
        share = [d * outer_n + o for o in share_outer for d in share_dp]
        got = lax.all_to_all(pieces, BOTH, 0, 0, axis_index_groups=[share], tiled=True)
        m_part, v_part = call(
            prep_kernel, [near_shape(tall, f32)] * 2,
            [dense(m_codes), dense(v_codes), m_scales, v_scales],
        )
        piece, square = call(
            lambda *refs: sum_kernel(count, rows, *refs),
            [near_shape(got.shape[1:], f32), shape_of((total_n, 1, LANES), f32)],
            [near(got)],
        )
        squares = lax.all_to_all(square, BOTH, 0, 0, tiled=True)
        held = {0: piece}
        bit = outer_n // 2
        while bit:
            for at in list(held):
                held[at ^ bit] = flip(held[at], outer_n, bit)
            bit //= 2
        args = [squares, dense(master), m_part, v_part] + [held[i] for i in range(outer_n)]
        args = [near(a) for a in args]
        (mine,) = call(
            lambda *refs: weight_kernel(rows, *refs),
            [near_shape((dp_n, rows * tiles, LANES), bf16)], args,
            scratch_shapes=[pltpu.VMEM((outer_n, part * rows, LANES), f32)],
        )
        spread = ordered(dp_n, SPREAD_EIGHTHS)
        mine = lax.all_to_all(mine, "dp", 0, 0, axis_index_groups=[spread], tiled=True)
        mine = arrange(mine, inverse(SPREAD_EIGHTHS)).reshape(rows_all, width)
        half_spec = vmem if is_small(mine) else far
        other = flip(mine, outer_n, 1)
        fresh, m_next, v_next, m_top, v_top = call(
            lambda *refs: state_kernel(rows, *refs),
            [
                shape_of(tall, f32), shape_of(tall, bf16), shape_of(tall, bf16),
                shape_of(m_scales.shape, f32), shape_of(v_scales.shape, f32),
            ],
            args,
        )
        (weights,) = call(
            halves_kernel, [shape_of(own.shape, bf16)], [near(mine), near(other)],
            in_specs=[half_spec] * 2, out_specs=[far],
            scratch_shapes=[pltpu.SemaphoreType.DMA((2,))],
        )
        return (plain(fresh, rows), plain(m_next, rows), plain(v_next, rows), m_top, v_top, weights)

    return body


def solution(mesh):
    rows = P(None, "dp", None)
    outer_n = mesh.shape["outer"]
    return jax.shard_map(
        make_body(mesh.shape["dp"], outer_n),
        mesh=mesh,
        in_specs=(P("outer", "dp", None, None, None), rows, rows, rows, rows, rows),
        out_specs=(rows, rows, rows, rows, rows, P()),
        check_vma=False,
    )
```

```python
import jax
import jax.numpy as jnp
from jax import lax
from jax.experimental import pallas as pl
from jax.experimental.pallas import tpu as pltpu
from jax.sharding import PartitionSpec as P

BLOCK = 2048
STEP = 10
LANES = 128
SUBLANES = 8
NEAR_BYTES = 768 * 1024
BOTH = ("dp", "outer")
FIRST_FIX = 1.0 / (1.0 - 0.9**STEP)
SECOND_FIX = 1.0 / (1.0 - 0.95**STEP)
SPREAD_EIGHTHS = (2, 7, 6, 1, 0, 5, 3, 4)
SHARE_EIGHTHS = (2, 3, 0, 4, 5, 6, 1, 7)
SHARE_QUARTERS = (3, 1, 0, 2)


def ordered(size, parts):
    if size % len(parts):
        return list(range(size))
    span = size // len(parts)
    return [part * span + i for part in parts for i in range(span)]


def arrange(value, parts):
    if value.shape[0] % len(parts):
        return value
    blocks = jnp.split(value, len(parts), axis=0)
    return jnp.concatenate([blocks[part] for part in parts], axis=0)


def inverse(parts):
    return tuple(parts.index(i) for i in range(len(parts)))


def sum_kernel(got_ref, v_ref, ms_ref, vs_ref, piece_ref, square_ref, scale_ref, v_out_ref):
    count, rows, blocks = ms_ref.shape
    span = BLOCK // LANES * rows
    for at in range(count):
        for block in range(blocks):
            here = pl.ds(block * span, span)
            v_out_ref[at, here, :] = 0.95 * scaled_rows(v_ref[at, here, :], scale_rows(vs_ref, at, block, rows))
            wide = jnp.broadcast_to(scale_rows(ms_ref, at, block, rows), (SUBLANES, LANES))
            scale_ref[at, block] = wide
    terms = got_ref.shape[0]
    group = 8

    def some(i):
        return jnp.sum(got_ref[pl.ds(i * group, group)].astype(jnp.float32), axis=0)

    total = some(0)
    if terms <= 4 * group:
        for i in range(1, terms // group):
            total = total + some(i)
    else:
        total = lax.fori_loop(1, terms // group, lambda i, held: held + some(i), total)
    part = total.shape[0] // (count * rows)
    for at in range(count):
        for row in range(rows):
            start = (at * rows + row) * part
            piece_ref[pl.ds(at * rows * part + row, part, stride=rows), :] = total[start : start + part]
    lanes = jnp.sum(total * total, axis=0, keepdims=True)
    square_ref[...] = jnp.broadcast_to(lanes[None], square_ref.shape)


def scale_rows(scale_ref, at, block, rows):
    scale = scale_ref[at, :, block : block + 1]
    return jnp.concatenate([scale] * (SUBLANES // rows), axis=0)


def scaled_rows(codes, scale):
    tiles = codes.astype(jnp.float32).reshape(codes.shape[0] // SUBLANES, SUBLANES, LANES)
    return (tiles * scale).reshape(codes.shape)


def clip_of(square_ref):
    total = jnp.sum(jnp.sum(square_ref[...], axis=0), axis=1, keepdims=True)
    return 1.0 / jnp.maximum(jnp.sqrt(total), 1.0)


def moments(clip, piece_ref, m_ref, scale_ref, v_ref, at, start, block, span):
    here = pl.ds(pl.multiple_of(block * span, SUBLANES), span)
    g = clip * piece_ref[pl.ds(start, span), :]
    m = 0.9 * scaled_rows(m_ref[at, here, :], scale_ref[at, block]) + 0.1 * g
    return m, v_ref[at, here, :] + 0.05 * g * g, here


def fresh_of(master_ref, at, here, m, v):
    update = (m * FIRST_FIX) / (jnp.sqrt(v * SECOND_FIX) + 1e-08)
    return master_ref[at, here, :] - 0.01 * update


def weight_kernel(rows, square_ref, master_ref, m_ref, scale_ref, v_ref, *refs):
    *piece_refs, out_ref, hold_ref = refs
    outer_at = lax.axis_index("outer")
    side = outer_at % 2
    held = piece_refs[0].shape[0] // master_ref.shape[0]
    span = BLOCK // LANES * rows
    part = span // rows
    clip = clip_of(square_ref)
    for offset, piece_ref in enumerate(piece_refs):
        for inner in range(held // span):
            block = (outer_at ^ offset) * (held // span) + inner
            start = pl.multiple_of(side * held + inner * span, SUBLANES)
            m, v, here = moments(clip, piece_ref, m_ref, scale_ref, v_ref, side, start, block, span)
            hold_ref[offset, inner] = fresh_of(master_ref, side, here, m, v)
            for row in range(rows):
                fresh = hold_ref[offset, inner, pl.ds(row, part, stride=rows), :].astype(jnp.bfloat16)
                at = row * (out_ref.shape[1] // rows) + block * part
                there = pl.ds(pl.multiple_of(at, SUBLANES), part)
                out_ref[:, there, :] = jnp.broadcast_to(fresh[None], (out_ref.shape[0],) + fresh.shape)


def half_copy(half_ref, weights_ref, side, sem):
    return pltpu.make_async_copy(half_ref, weights_ref.at[side], sem)


def halves_kernel(mine_ref, other_ref, out_ref, sems):
    side = lax.axis_index("outer") % 2
    copies = [
        half_copy(mine_ref, out_ref, side, sems.at[0]),
        half_copy(other_ref, out_ref, 1 - side, sems.at[1]),
    ]
    for copy in copies:
        copy.start()
    for copy in copies:
        copy.wait()


def state_kernel(rows, square_ref, master_ref, m_ref, scale_ref, v_ref, *refs):
    *piece_refs, fresh_ref, m_next_ref, v_next_ref, m_top_ref, v_top_ref = refs
    outer_at = lax.axis_index("outer")
    count = master_ref.shape[0]
    span = BLOCK // LANES * rows
    held = piece_refs[0].shape[0] // count
    clip = clip_of(square_ref)
    columns = lax.broadcasted_iota(jnp.int32, m_top_ref.shape[1:], 1)

    def top_of(value):
        top = jnp.max(jnp.abs(value).reshape(span // SUBLANES, SUBLANES, LANES), axis=0)
        step = rows
        while step < SUBLANES:
            top = jnp.maximum(top, pltpu.roll(top, step, 0))
            step *= 2
        return jnp.max(top, axis=1, keepdims=True) + 1e-20

    def scaled(value, top):
        tiles = value.reshape(span // SUBLANES, SUBLANES, LANES)
        return (tiles * (1.0 / top)).reshape(span, LANES).astype(jnp.bfloat16)

    for at in range(count):
        m_tops = v_tops = jnp.zeros(m_top_ref.shape[1:], jnp.float32)
        for offset, piece_ref in enumerate(piece_refs):
            for inner in range(held // span):
                block = (outer_at ^ offset) * (held // span) + inner
                start = at * held + inner * span
                m, v, here = moments(clip, piece_ref, m_ref, scale_ref, v_ref, at, start, block, span)
                fresh_ref[at, here, :] = fresh_of(master_ref, at, here, m, v)
                m_top, v_top = top_of(m), top_of(v)
                m_next_ref[at, here, :] = scaled(m, m_top)
                v_next_ref[at, here, :] = scaled(v, v_top)
                m_tops = jnp.where(columns == block, m_top[:rows], m_tops)
                v_tops = jnp.where(columns == block, v_top[:rows], v_tops)
        m_top_ref[at] = m_tops
        v_top_ref[at] = v_tops


def is_small(value):
    return value.size * value.dtype.itemsize <= NEAR_BYTES


def near(value):
    return pltpu.with_memory_space_constraint(value, pltpu.VMEM) if is_small(value) else value


def call(kernel, outs, args, in_specs=None, out_specs=None, **extra):
    spec = pl.BlockSpec(memory_space=pltpu.VMEM)
    return pl.pallas_call(
        kernel,
        out_shape=outs,
        in_specs=in_specs or [spec] * len(args),
        out_specs=out_specs or [spec] * len(outs),
        **extra,
    )(*args)


def near_shape(shape, dtype):
    far = jax.ShapeDtypeStruct(shape, dtype)
    return pltpu.VMEM(shape, dtype) if is_small(far) else far


def dense(value):
    count, rows, width = value.shape
    tiles = value.reshape(count, rows, width // LANES, LANES).transpose(0, 2, 1, 3)
    return tiles.reshape(count, width // LANES * rows, LANES)


def plain(value, rows):
    count, tall, lanes = value.shape
    tiles = value.reshape(count, tall // rows, rows, lanes).transpose(0, 2, 1, 3)
    return tiles.reshape(count, rows, tall // rows * lanes)


def flip(value, size, bit):
    return lax.ppermute(value, "outer", [(i, i ^ bit) for i in range(size)])


def make_body(dp_n, outer_n):
    f32, bf16 = jnp.float32, jnp.bfloat16

    def body(partials, master, m_codes, v_codes, m_scales, v_scales):
        own = partials[0, 0]
        count, rows_all, width = own.shape
        rows = rows_all // dp_n
        total_n = dp_n * outer_n
        tiles = width // LANES
        part = tiles // outer_n
        tall = (count, tiles * rows, LANES)
        vmem, far = pl.BlockSpec(memory_space=pltpu.VMEM), pl.BlockSpec(memory_space=pl.ANY)
        shape_of = jax.ShapeDtypeStruct
        pieces = own.reshape(count, dp_n, rows, outer_n, part, LANES)
        pieces = arrange(pieces.transpose(1, 3, 0, 2, 4, 5), SHARE_EIGHTHS)
        pieces = arrange(pieces.transpose(1, 0, 2, 3, 4, 5), SHARE_QUARTERS)
        pieces = pieces.reshape(total_n, count * rows * part, LANES)
        share_dp, share_outer = ordered(dp_n, SHARE_EIGHTHS), ordered(outer_n, SHARE_QUARTERS)
        share = [d * outer_n + o for o in share_outer for d in share_dp]
        got = lax.all_to_all(pieces, BOTH, 0, 0, axis_index_groups=[share], tiled=True)
        blocks = m_scales.shape[2]
        piece, square, scales, v_part = call(
            sum_kernel,
            [
                near_shape(got.shape[1:], f32), shape_of((total_n, 1, LANES), f32),
                near_shape((count, blocks, SUBLANES, LANES), f32), near_shape(tall, f32),
            ],
            [near(a) for a in (got, dense(v_codes), m_scales, v_scales)],
        )
        squares = lax.all_to_all(square, BOTH, 0, 0, tiled=True)
        held = {0: piece}
        for at in range(outer_n - 1, 0, -1):
            held[at] = flip(piece, outer_n, at)
        args = [squares, dense(master), dense(m_codes), scales, v_part] + [held[i] for i in range(outer_n)]
        args = [near(a) for a in args]
        (mine,) = call(
            lambda *refs: weight_kernel(rows, *refs),
            [near_shape((dp_n, rows * tiles, LANES), bf16)], args,
            scratch_shapes=[pltpu.VMEM((outer_n, blocks // outer_n, tiles // blocks * rows, LANES), f32)],
        )
        spread = ordered(dp_n, SPREAD_EIGHTHS)
        mine = lax.all_to_all(mine, "dp", 0, 0, axis_index_groups=[spread], tiled=True)
        mine = arrange(mine, inverse(SPREAD_EIGHTHS)).reshape(rows_all, width)
        half_spec = vmem if is_small(mine) else far
        other = flip(mine, outer_n, 1)
        fresh, m_next, v_next, m_top, v_top = call(
            lambda *refs: state_kernel(rows, *refs),
            [
                shape_of(tall, f32), shape_of(tall, bf16), shape_of(tall, bf16),
                shape_of(m_scales.shape, f32), shape_of(v_scales.shape, f32),
            ],
            args,
        )
        (weights,) = call(
            halves_kernel, [shape_of(own.shape, bf16)], [near(mine), near(other)],
            in_specs=[half_spec] * 2, out_specs=[far],
            scratch_shapes=[pltpu.SemaphoreType.DMA((2,))],
        )
        return (plain(fresh, rows), plain(m_next, rows), plain(v_next, rows), m_top, v_top, weights)

    return body


def solution(mesh):
    rows = P(None, "dp", None)
    outer_n = mesh.shape["outer"]
    return jax.shard_map(
        make_body(mesh.shape["dp"], outer_n),
        mesh=mesh,
        in_specs=(P("outer", "dp", None, None, None), rows, rows, rows, rows, rows),
        out_specs=(rows, rows, rows, rows, rows, P()),
        check_vma=False,
    )
```

```python
import jax
import jax.numpy as jnp
from jax import lax
from jax.experimental import pallas as pl
from jax.experimental.pallas import tpu as pltpu
from jax.sharding import PartitionSpec as P

BLOCK = 2048
STEP = 10
LANES = 128
SUBLANES = 8
NEAR_BYTES = 768 * 1024
BOTH = ("dp", "outer")
FIRST_FIX = 1.0 / (1.0 - 0.9**STEP)
SECOND_FIX = 1.0 / (1.0 - 0.95**STEP)
SPREAD_EIGHTHS = (2, 7, 6, 1, 0, 5, 3, 4)
SHARE_EIGHTHS = (2, 3, 0, 4, 5, 6, 1, 7)
SHARE_QUARTERS = (3, 1, 0, 2)


def ordered(size, parts):
    if size % len(parts):
        return list(range(size))
    span = size // len(parts)
    return [part * span + i for part in parts for i in range(span)]


def arrange(value, parts):
    if value.shape[0] % len(parts):
        return value
    blocks = jnp.split(value, len(parts), axis=0)
    return jnp.concatenate([blocks[part] for part in parts], axis=0)


def inverse(parts):
    return tuple(parts.index(i) for i in range(len(parts)))


def cut_kernel(places, rows, own_ref, pieces_ref):
    count = own_ref.shape[0]
    part = pieces_ref.shape[1] // (count * rows)
    for place, (d, o) in enumerate(places):
        for at in range(count):
            for row in range(rows):
                there = pl.ds((at * rows + row) * part, part)
                pieces_ref[place, there, :] = own_ref[at, d * rows + row, pl.ds(o * part, part), :]


def sum_kernel(got_ref, v_ref, ms_ref, vs_ref, piece_ref, square_ref, scale_ref, v_out_ref):
    count, rows, blocks = ms_ref.shape
    span = BLOCK // LANES * rows
    for at in range(count):
        for block in range(blocks):
            here = pl.ds(block * span, span)
            v_out_ref[at, here, :] = 0.95 * scaled_rows(v_ref[at, here, :], scale_rows(vs_ref, at, block, rows))
            wide = jnp.broadcast_to(scale_rows(ms_ref, at, block, rows), (SUBLANES, LANES))
            scale_ref[at, block] = wide
    terms = got_ref.shape[0]
    group = 8

    def some(i):
        return jnp.sum(got_ref[pl.ds(i * group, group)].astype(jnp.float32), axis=0)

    total = some(0)
    if terms <= 4 * group:
        for i in range(1, terms // group):
            total = total + some(i)
    else:
        total = lax.fori_loop(1, terms // group, lambda i, held: held + some(i), total)
    part = total.shape[0] // (count * rows)
    for at in range(count):
        for row in range(rows):
            start = (at * rows + row) * part
            piece_ref[pl.ds(at * rows * part + row, part, stride=rows), :] = total[start : start + part]
    lanes = jnp.sum(total * total, axis=0, keepdims=True)
    square_ref[...] = jnp.broadcast_to(lanes[None], square_ref.shape)


def scale_rows(scale_ref, at, block, rows):
    scale = scale_ref[at, :, block : block + 1]
    return jnp.concatenate([scale] * (SUBLANES // rows), axis=0)


def scaled_rows(codes, scale):
    tiles = codes.astype(jnp.float32).reshape(codes.shape[0] // SUBLANES, SUBLANES, LANES)
    return (tiles * scale).reshape(codes.shape)


def clip_of(square_ref):
    total = jnp.sum(jnp.sum(square_ref[...], axis=0), axis=1, keepdims=True)
    return 1.0 / jnp.maximum(jnp.sqrt(total), 1.0)


def moments(clip, piece_ref, m_ref, scale_ref, v_ref, at, start, block, span):
    here = pl.ds(pl.multiple_of(block * span, SUBLANES), span)
    g = clip * piece_ref[pl.ds(start, span), :]
    m = 0.9 * scaled_rows(m_ref[at, here, :], scale_ref[at, block]) + 0.1 * g
    return m, v_ref[at, here, :] + 0.05 * g * g, here


def fresh_of(master_ref, at, here, m, v):
    update = (m * FIRST_FIX) / (jnp.sqrt(v * SECOND_FIX) + 1e-08)
    return master_ref[at, here, :] - 0.01 * update


def weight_kernel(rows, square_ref, master_ref, m_ref, scale_ref, v_ref, *refs):
    *piece_refs, out_ref, hold_ref = refs
    outer_at = lax.axis_index("outer")
    side = outer_at % 2
    held = piece_refs[0].shape[0] // master_ref.shape[0]
    span = BLOCK // LANES * rows
    part = span // rows
    clip = clip_of(square_ref)
    for offset, piece_ref in enumerate(piece_refs):
        for inner in range(held // span):
            block = (outer_at ^ offset) * (held // span) + inner
            start = pl.multiple_of(side * held + inner * span, SUBLANES)
            m, v, here = moments(clip, piece_ref, m_ref, scale_ref, v_ref, side, start, block, span)
            hold_ref[offset, inner] = fresh_of(master_ref, side, here, m, v)
            for row in range(rows):
                fresh = hold_ref[offset, inner, pl.ds(row, part, stride=rows), :].astype(jnp.bfloat16)
                at = row * (out_ref.shape[1] // rows) + block * part
                there = pl.ds(pl.multiple_of(at, SUBLANES), part)
                out_ref[:, there, :] = jnp.broadcast_to(fresh[None], (out_ref.shape[0],) + fresh.shape)


def half_copy(half_ref, weights_ref, side, sem):
    return pltpu.make_async_copy(half_ref, weights_ref.at[side], sem)


def halves_kernel(mine_ref, other_ref, out_ref, sems):
    side = lax.axis_index("outer") % 2
    copies = [
        half_copy(mine_ref, out_ref, side, sems.at[0]),
        half_copy(other_ref, out_ref, 1 - side, sems.at[1]),
    ]
    for copy in copies:
        copy.start()
    for copy in copies:
        copy.wait()


def state_kernel(rows, square_ref, master_ref, m_ref, scale_ref, v_ref, *refs):
    *piece_refs, fresh_ref, m_next_ref, v_next_ref, m_top_ref, v_top_ref = refs
    outer_at = lax.axis_index("outer")
    count = master_ref.shape[0]
    span = BLOCK // LANES * rows
    held = piece_refs[0].shape[0] // count
    clip = clip_of(square_ref)
    columns = lax.broadcasted_iota(jnp.int32, m_top_ref.shape[1:], 1)

    def top_of(value):
        top = jnp.max(jnp.abs(value).reshape(span // SUBLANES, SUBLANES, LANES), axis=0)
        step = rows
        while step < SUBLANES:
            top = jnp.maximum(top, pltpu.roll(top, step, 0))
            step *= 2
        return jnp.max(top, axis=1, keepdims=True) + 1e-20

    def scaled(value, top):
        tiles = value.reshape(span // SUBLANES, SUBLANES, LANES)
        return (tiles * (1.0 / top)).reshape(span, LANES).astype(jnp.bfloat16)

    for at in range(count):
        m_tops = v_tops = jnp.zeros(m_top_ref.shape[1:], jnp.float32)
        for offset, piece_ref in enumerate(piece_refs):
            for inner in range(held // span):
                block = (outer_at ^ offset) * (held // span) + inner
                start = at * held + inner * span
                m, v, here = moments(clip, piece_ref, m_ref, scale_ref, v_ref, at, start, block, span)
                fresh_ref[at, here, :] = fresh_of(master_ref, at, here, m, v)
                m_top, v_top = top_of(m), top_of(v)
                m_next_ref[at, here, :] = scaled(m, m_top)
                v_next_ref[at, here, :] = scaled(v, v_top)
                m_tops = jnp.where(columns == block, m_top[:rows], m_tops)
                v_tops = jnp.where(columns == block, v_top[:rows], v_tops)
        m_top_ref[at] = m_tops
        v_top_ref[at] = v_tops


def is_small(value):
    return value.size * value.dtype.itemsize <= NEAR_BYTES


def near(value):
    return pltpu.with_memory_space_constraint(value, pltpu.VMEM) if is_small(value) else value


def call(kernel, outs, args, in_specs=None, out_specs=None, **extra):
    spec = pl.BlockSpec(memory_space=pltpu.VMEM)
    return pl.pallas_call(
        kernel,
        out_shape=outs,
        in_specs=in_specs or [spec] * len(args),
        out_specs=out_specs or [spec] * len(outs),
        **extra,
    )(*args)


def near_shape(shape, dtype):
    far = jax.ShapeDtypeStruct(shape, dtype)
    return pltpu.VMEM(shape, dtype) if is_small(far) else far


def dense(value):
    count, rows, width = value.shape
    tiles = value.reshape(count, rows, width // LANES, LANES).transpose(0, 2, 1, 3)
    return tiles.reshape(count, width // LANES * rows, LANES)


def plain(value, rows):
    count, tall, lanes = value.shape
    tiles = value.reshape(count, tall // rows, rows, lanes).transpose(0, 2, 1, 3)
    return tiles.reshape(count, rows, tall // rows * lanes)


def flip(value, size, bit):
    return lax.ppermute(value, "outer", [(i, i ^ bit) for i in range(size)])


def make_body(dp_n, outer_n):
    f32, bf16 = jnp.float32, jnp.bfloat16

    def body(partials, master, m_codes, v_codes, m_scales, v_scales):
        own = partials[0, 0]
        count, rows_all, width = own.shape
        rows = rows_all // dp_n
        total_n = dp_n * outer_n
        tiles = width // LANES
        part = tiles // outer_n
        tall = (count, tiles * rows, LANES)
        vmem, far = pl.BlockSpec(memory_space=pltpu.VMEM), pl.BlockSpec(memory_space=pl.ANY)
        shape_of = jax.ShapeDtypeStruct
        share_dp, share_outer = ordered(dp_n, SHARE_EIGHTHS), ordered(outer_n, SHARE_QUARTERS)
        places = [(d, o) for o in share_outer for d in share_dp]
        share = [d * outer_n + o for d, o in places]
        (pieces,) = call(
            lambda *refs: cut_kernel(places, rows, *refs),
            [near_shape((total_n, count * rows * part, LANES), bf16)],
            [near(own.reshape(count, rows_all, tiles, LANES))],
        )
        got = lax.all_to_all(pieces, BOTH, 0, 0, axis_index_groups=[share], tiled=True)
        blocks = m_scales.shape[2]
        piece, square, scales, v_part = call(
            sum_kernel,
            [
                near_shape(got.shape[1:], f32), shape_of((total_n, 1, LANES), f32),
                near_shape((count, blocks, SUBLANES, LANES), f32), near_shape(tall, f32),
            ],
            [near(a) for a in (got, dense(v_codes), m_scales, v_scales)],
        )
        squares = lax.all_to_all(square, BOTH, 0, 0, tiled=True)
        held = {0: piece}
        for at in range(outer_n - 1, 0, -1):
            held[at] = flip(piece, outer_n, at)
        args = [squares, dense(master), dense(m_codes), scales, v_part] + [held[i] for i in range(outer_n)]
        args = [near(a) for a in args]
        (mine,) = call(
            lambda *refs: weight_kernel(rows, *refs),
            [near_shape((dp_n, rows * tiles, LANES), bf16)], args,
            scratch_shapes=[pltpu.VMEM((outer_n, blocks // outer_n, tiles // blocks * rows, LANES), f32)],
        )
        spread = ordered(dp_n, SPREAD_EIGHTHS)
        mine = lax.all_to_all(mine, "dp", 0, 0, axis_index_groups=[spread], tiled=True)
        mine = arrange(mine, inverse(SPREAD_EIGHTHS)).reshape(rows_all, width)
        half_spec = vmem if is_small(mine) else far
        other = flip(mine, outer_n, 1)
        fresh, m_next, v_next, m_top, v_top = call(
            lambda *refs: state_kernel(rows, *refs),
            [
                shape_of(tall, f32), shape_of(tall, bf16), shape_of(tall, bf16),
                shape_of(m_scales.shape, f32), shape_of(v_scales.shape, f32),
            ],
            args,
        )
        (weights,) = call(
            halves_kernel, [shape_of(own.shape, bf16)], [near(mine), near(other)],
            in_specs=[half_spec] * 2, out_specs=[far],
            scratch_shapes=[pltpu.SemaphoreType.DMA((2,))],
        )
        return (plain(fresh, rows), plain(m_next, rows), plain(v_next, rows), m_top, v_top, weights)

    return body


def solution(mesh):
    rows = P(None, "dp", None)
    outer_n = mesh.shape["outer"]
    return jax.shard_map(
        make_body(mesh.shape["dp"], outer_n),
        mesh=mesh,
        in_specs=(P("outer", "dp", None, None, None), rows, rows, rows, rows, rows),
        out_specs=(rows, rows, rows, rows, rows, P()),
        check_vma=False,
    )
```

```python
import jax
import jax.numpy as jnp
from jax import lax
from jax.experimental import pallas as pl
from jax.experimental.pallas import tpu as pltpu
from jax.sharding import PartitionSpec as P

BLOCK = 2048
STEP = 10
LANES = 128
SUBLANES = 8
NEAR_BYTES = 768 * 1024
BOTH = ("dp", "outer")
FIRST_FIX = 1.0 / (1.0 - 0.9**STEP)
SECOND_FIX = 1.0 / (1.0 - 0.95**STEP)
SPREAD_EIGHTHS = (2, 7, 6, 1, 0, 5, 3, 4)
SHARE_EIGHTHS = (2, 3, 0, 4, 5, 6, 1, 7)
SHARE_QUARTERS = (3, 1, 0, 2)


def ordered(size, parts):
    if size % len(parts):
        return list(range(size))
    span = size // len(parts)
    return [part * span + i for part in parts for i in range(span)]


def cut_kernel(places, rows, own_ref, pieces_ref):
    count = own_ref.shape[0]
    part = pieces_ref.shape[1] // (count * rows)
    for place, (d, o) in enumerate(places):
        for at in range(count):
            for row in range(rows):
                there = pl.ds((at * rows + row) * part, part)
                pieces_ref[place, there, :] = own_ref[at, d * rows + row, pl.ds(o * part, part), :]


def line_up_kernel(order, got_ref, lined_ref):
    for place, member in enumerate(order):
        lined_ref[member] = got_ref[place]


def sum_kernel(got_ref, v_ref, ms_ref, vs_ref, piece_ref, square_ref, scale_ref, v_out_ref):
    count, rows, blocks = ms_ref.shape
    span = BLOCK // LANES * rows
    for at in range(count):
        for block in range(blocks):
            here = pl.ds(block * span, span)
            v_out_ref[at, here, :] = 0.95 * scaled_rows(v_ref[at, here, :], scale_rows(vs_ref, at, block, rows))
            wide = jnp.broadcast_to(scale_rows(ms_ref, at, block, rows), (SUBLANES, LANES))
            scale_ref[at, block] = wide
    terms = got_ref.shape[0]
    group = 8

    def some(i):
        return jnp.sum(got_ref[pl.ds(i * group, group)].astype(jnp.float32), axis=0)

    total = some(0)
    if terms <= 4 * group:
        for i in range(1, terms // group):
            total = total + some(i)
    else:
        total = lax.fori_loop(1, terms // group, lambda i, held: held + some(i), total)
    part = total.shape[0] // (count * rows)
    for at in range(count):
        for row in range(rows):
            start = (at * rows + row) * part
            piece_ref[pl.ds(at * rows * part + row, part, stride=rows), :] = total[start : start + part]
    lanes = jnp.sum(total * total, axis=0, keepdims=True)
    square_ref[...] = jnp.broadcast_to(lanes[None], square_ref.shape)


def scale_rows(scale_ref, at, block, rows):
    scale = scale_ref[at, :, block : block + 1]
    return jnp.concatenate([scale] * (SUBLANES // rows), axis=0)


def scaled_rows(codes, scale):
    tiles = codes.astype(jnp.float32).reshape(codes.shape[0] // SUBLANES, SUBLANES, LANES)
    return (tiles * scale).reshape(codes.shape)


def clip_of(square_ref):
    total = jnp.sum(jnp.sum(square_ref[...], axis=0), axis=1, keepdims=True)
    return 1.0 / jnp.maximum(jnp.sqrt(total), 1.0)


def moments(clip, piece_ref, m_ref, scale_ref, v_ref, at, start, block, span):
    here = pl.ds(pl.multiple_of(block * span, SUBLANES), span)
    g = clip * piece_ref[pl.ds(start, span), :]
    m = 0.9 * scaled_rows(m_ref[at, here, :], scale_ref[at, block]) + 0.1 * g
    return m, v_ref[at, here, :] + 0.05 * g * g, here


def fresh_of(master_ref, at, here, m, v):
    update = (m * FIRST_FIX) / (jnp.sqrt(v * SECOND_FIX) + 1e-08)
    return master_ref[at, here, :] - 0.01 * update


def weight_kernel(rows, square_ref, master_ref, m_ref, scale_ref, v_ref, *refs):
    *piece_refs, out_ref, hold_ref = refs
    outer_at = lax.axis_index("outer")
    side = outer_at % 2
    held = piece_refs[0].shape[0] // master_ref.shape[0]
    span = BLOCK // LANES * rows
    part = span // rows
    clip = clip_of(square_ref)
    for offset, piece_ref in enumerate(piece_refs):
        for inner in range(held // span):
            block = (outer_at ^ offset) * (held // span) + inner
            start = pl.multiple_of(side * held + inner * span, SUBLANES)
            m, v, here = moments(clip, piece_ref, m_ref, scale_ref, v_ref, side, start, block, span)
            hold_ref[offset, inner] = fresh_of(master_ref, side, here, m, v)
            for row in range(rows):
                fresh = hold_ref[offset, inner, pl.ds(row, part, stride=rows), :].astype(jnp.bfloat16)
                at = row * (out_ref.shape[1] // rows) + block * part
                there = pl.ds(pl.multiple_of(at, SUBLANES), part)
                out_ref[:, there, :] = jnp.broadcast_to(fresh[None], (out_ref.shape[0],) + fresh.shape)


def half_copy(half_ref, weights_ref, side, sem):
    return pltpu.make_async_copy(half_ref, weights_ref.at[side], sem)


def halves_kernel(mine_ref, other_ref, out_ref, sems):
    side = lax.axis_index("outer") % 2
    copies = [
        half_copy(mine_ref, out_ref, side, sems.at[0]),
        half_copy(other_ref, out_ref, 1 - side, sems.at[1]),
    ]
    for copy in copies:
        copy.start()
    for copy in copies:
        copy.wait()


def state_kernel(rows, square_ref, master_ref, m_ref, scale_ref, v_ref, *refs):
    *piece_refs, fresh_ref, m_next_ref, v_next_ref, m_top_ref, v_top_ref = refs
    outer_at = lax.axis_index("outer")
    count = master_ref.shape[0]
    span = BLOCK // LANES * rows
    held = piece_refs[0].shape[0] // count
    clip = clip_of(square_ref)
    columns = lax.broadcasted_iota(jnp.int32, m_top_ref.shape[1:], 1)

    def top_of(value):
        top = jnp.max(jnp.abs(value).reshape(span // SUBLANES, SUBLANES, LANES), axis=0)
        step = rows
        while step < SUBLANES:
            top = jnp.maximum(top, pltpu.roll(top, step, 0))
            step *= 2
        return jnp.max(top, axis=1, keepdims=True) + 1e-20

    def scaled(value, top):
        tiles = value.reshape(span // SUBLANES, SUBLANES, LANES)
        return (tiles * (1.0 / top)).reshape(span, LANES).astype(jnp.bfloat16)

    for at in range(count):
        m_tops = v_tops = jnp.zeros(m_top_ref.shape[1:], jnp.float32)
        for offset, piece_ref in enumerate(piece_refs):
            for inner in range(held // span):
                block = (outer_at ^ offset) * (held // span) + inner
                start = at * held + inner * span
                m, v, here = moments(clip, piece_ref, m_ref, scale_ref, v_ref, at, start, block, span)
                fresh_ref[at, here, :] = fresh_of(master_ref, at, here, m, v)
                m_top, v_top = top_of(m), top_of(v)
                m_next_ref[at, here, :] = scaled(m, m_top)
                v_next_ref[at, here, :] = scaled(v, v_top)
                m_tops = jnp.where(columns == block, m_top[:rows], m_tops)
                v_tops = jnp.where(columns == block, v_top[:rows], v_tops)
        m_top_ref[at] = m_tops
        v_top_ref[at] = v_tops


def is_small(value):
    return value.size * value.dtype.itemsize <= NEAR_BYTES


def near(value):
    return pltpu.with_memory_space_constraint(value, pltpu.VMEM) if is_small(value) else value


def call(kernel, outs, args, in_specs=None, out_specs=None, **extra):
    spec = pl.BlockSpec(memory_space=pltpu.VMEM)
    return pl.pallas_call(
        kernel,
        out_shape=outs,
        in_specs=in_specs or [spec] * len(args),
        out_specs=out_specs or [spec] * len(outs),
        **extra,
    )(*args)


def near_shape(shape, dtype):
    far = jax.ShapeDtypeStruct(shape, dtype)
    return pltpu.VMEM(shape, dtype) if is_small(far) else far


def dense(value):
    count, rows, width = value.shape
    tiles = value.reshape(count, rows, width // LANES, LANES).transpose(0, 2, 1, 3)
    return tiles.reshape(count, width // LANES * rows, LANES)


def plain(value, rows):
    count, tall, lanes = value.shape
    tiles = value.reshape(count, tall // rows, rows, lanes).transpose(0, 2, 1, 3)
    return tiles.reshape(count, rows, tall // rows * lanes)


def flip(value, size, bit):
    return lax.ppermute(value, "outer", [(i, i ^ bit) for i in range(size)])


def make_body(dp_n, outer_n):
    f32, bf16 = jnp.float32, jnp.bfloat16

    def body(partials, master, m_codes, v_codes, m_scales, v_scales):
        own = partials[0, 0]
        count, rows_all, width = own.shape
        rows = rows_all // dp_n
        total_n = dp_n * outer_n
        tiles = width // LANES
        part = tiles // outer_n
        tall = (count, tiles * rows, LANES)
        vmem, far = pl.BlockSpec(memory_space=pltpu.VMEM), pl.BlockSpec(memory_space=pl.ANY)
        shape_of = jax.ShapeDtypeStruct
        share_dp, share_outer = ordered(dp_n, SHARE_EIGHTHS), ordered(outer_n, SHARE_QUARTERS)
        places = [(d, o) for o in share_outer for d in share_dp]
        share = [d * outer_n + o for d, o in places]
        (pieces,) = call(
            lambda *refs: cut_kernel(places, rows, *refs),
            [near_shape((total_n, count * rows * part, LANES), bf16)],
            [near(own.reshape(count, rows_all, tiles, LANES))],
        )
        got = lax.all_to_all(pieces, BOTH, 0, 0, axis_index_groups=[share], tiled=True)
        blocks = m_scales.shape[2]
        piece, square, scales, v_part = call(
            sum_kernel,
            [
                near_shape(got.shape[1:], f32), shape_of((total_n, 1, LANES), f32),
                near_shape((count, blocks, SUBLANES, LANES), f32), near_shape(tall, f32),
            ],
            [near(a) for a in (got, dense(v_codes), m_scales, v_scales)],
        )
        squares = lax.all_to_all(square, BOTH, 0, 0, tiled=True)
        held = {0: piece}
        for at in range(outer_n - 1, 0, -1):
            held[at] = flip(piece, outer_n, at)
        args = [squares, dense(master), dense(m_codes), scales, v_part] + [held[i] for i in range(outer_n)]
        args = [near(a) for a in args]
        (mine,) = call(
            lambda *refs: weight_kernel(rows, *refs),
            [near_shape((dp_n, rows * tiles, LANES), bf16)], args,
            scratch_shapes=[pltpu.VMEM((outer_n, blocks // outer_n, tiles // blocks * rows, LANES), f32)],
        )
        spread = ordered(dp_n, SPREAD_EIGHTHS)
        mine = lax.all_to_all(mine, "dp", 0, 0, axis_index_groups=[spread], tiled=True)
        (mine,) = call(
            lambda *refs: line_up_kernel(spread, *refs),
            [near_shape(mine.shape, bf16)], [near(mine)],
        )
        mine = mine.reshape(rows_all, width)
        half_spec = vmem if is_small(mine) else far
        other = flip(mine, outer_n, 1)
        fresh, m_next, v_next, m_top, v_top = call(
            lambda *refs: state_kernel(rows, *refs),
            [
                shape_of(tall, f32), shape_of(tall, bf16), shape_of(tall, bf16),
                shape_of(m_scales.shape, f32), shape_of(v_scales.shape, f32),
            ],
            args,
        )
        (weights,) = call(
            halves_kernel, [shape_of(own.shape, bf16)], [near(mine), near(other)],
            in_specs=[half_spec] * 2, out_specs=[far],
            scratch_shapes=[pltpu.SemaphoreType.DMA((2,))],
        )
        return (plain(fresh, rows), plain(m_next, rows), plain(v_next, rows), m_top, v_top, weights)

    return body


def solution(mesh):
    rows = P(None, "dp", None)
    outer_n = mesh.shape["outer"]
    return jax.shard_map(
        make_body(mesh.shape["dp"], outer_n),
        mesh=mesh,
        in_specs=(P("outer", "dp", None, None, None), rows, rows, rows, rows, rows),
        out_specs=(rows, rows, rows, rows, rows, P()),
        check_vma=False,
    )
```
